128 devices in a mesh: dp: 8 (over z, y_lo), ctx: 16 (over y_hi, x, core).
Axes of the slice: x: 4, y: 4 (y_hi: 2, y_lo: 2; y = y_hi * 2 + y_lo), z: 4, core: 2. Of those that a mesh axis runs over, the one named last changes fastest.
Arguments:
- queries: bfloat16 [32768, 4096], P(('dp', 'ctx')), parts along dimension 0, may hold values from -5 to 5
- keys_values: bfloat16 [32768, 2, 1024], P(('dp', 'ctx')), parts along dimension 0, may hold values from -5 to 5
- fold: int32 [256], P('dp'), parts along dimension 0, may hold values from 0 to 31, each once
- doc_length: int32 [8], P('dp'), parts along dimension 0, may hold values from 2048 to 4096
Outputs:
- attended: bfloat16 [32768, 4096], P(('dp', 'ctx')), parts along dimension 0
The draws below stay inside these ranges and needn't reach their ends.
There are 8 independent parts, one for each index of `dp`. The reference program is written for one: setup_inputs(seed, part) draws one part's arguments, and reference() takes and returns one part's arrays. A program takes and returns all parts, laid end to end along the dimension named above; each array names one. Nothing has to cross between parts.
Inputs may be any that keep to these rules, and one draw needn't show every extreme that they name: A permutation: slot s, the stored rows s * 128 to (s + 1) * 128 - 1, holds positions fold[s] * 128 onwards. `doc_length`: positions at or beyond it are padding.
All inputs are finite; a program needn't handle non-finite values.
Results may differ from the reference program's by a relative error of at most 0.004.
Values may be sent and summed in bfloat16 or wider, within the bound.
A program may use at most 320 MiB of HBM per device.

```python
import math
import jax
import jax.numpy as jnp
from jax import lax

HEADS = 32
KV_HEADS = 8
HEAD_DIM = 128
SPAN = 128
SPANS = 32
TOKENS = 4096


def draw_queries(key, part):
    width = HEADS * HEAD_DIM
    result = jnp.clip(1.5 * jax.random.normal(jax.random.fold_in(key, 1), (TOKENS, width), jnp.float32), -5.0, 5.0)
    return result.astype(jnp.bfloat16)


def draw_keys_values(key, part):
    width = KV_HEADS * HEAD_DIM
    key_part = jnp.clip(1.5 * jax.random.normal(jax.random.fold_in(key, 2), (TOKENS, width), jnp.float32), -5.0, 5.0)
    value_part = jnp.clip(jax.random.normal(jax.random.fold_in(key, 3), (TOKENS, width), jnp.float32), -5.0, 5.0)
    return jnp.stack([key_part, value_part], axis=1).astype(jnp.bfloat16)


def setup_inputs(seed: int = 0, part: int = 0) -> dict:
    seeds = jax.random.split(jax.random.key(seed), 5)
    part_keys = jax.random.split(jax.random.fold_in(seeds[4], part), 5)
    queries = draw_queries(jax.random.fold_in(jax.random.fold_in(seeds[4], part), 71), part)
    keys_values = draw_keys_values(jax.random.fold_in(jax.random.fold_in(seeds[4], part), 71), part)
    fold = jax.random.permutation(part_keys[2], SPANS).astype(jnp.int32)
    doc_length = jax.random.randint(part_keys[3], (1,), TOKENS // 2, TOKENS + 1).astype(jnp.int32)
    return {"queries": queries, "keys_values": keys_values, "fold": fold, "doc_length": doc_length}


def positions(fold, row_count, span_rows):
    row_ids = jnp.arange(row_count, dtype=jnp.int32)
    slot_ids = (row_ids // span_rows).astype(jnp.int32)
    return fold[slot_ids] * span_rows + row_ids % span_rows

def reference(queries, keys_values, fold, doc_length):
    position = positions(fold, TOKENS, SPAN)
    length = doc_length[0]
    visible = (position[None, :] <= position[:, None]) & (position[None, :] < length)
    group_size = HEADS // KV_HEADS
    score_scale = 1.0 / math.sqrt(HEAD_DIM)
    query_heads = queries.reshape(TOKENS, KV_HEADS, group_size, HEAD_DIM).transpose(1, 2, 0, 3)
    key_heads = keys_values[:, 0].reshape(TOKENS, KV_HEADS, HEAD_DIM).transpose(1, 0, 2)
    value_heads = keys_values[:, 1].reshape(TOKENS, KV_HEADS, HEAD_DIM).transpose(1, 0, 2)

    def one_group(operands):
        query_group, key_block, value_block = operands

        def one_head(query_head):
            scores = jnp.dot(query_head, key_block.T, preferred_element_type=jnp.float32) * score_scale
            scores = jnp.where(visible, scores, -1e+30)
            row_max = lax.optimization_barrier(jnp.max(scores, axis=1, keepdims=True))
            weights = jnp.where(visible, jnp.exp(scores - row_max), 0.0)
            weight_sum = lax.optimization_barrier(jnp.sum(weights, axis=1, keepdims=True))
            numerator = jnp.dot(weights.astype(jnp.bfloat16), value_block, preferred_element_type=jnp.float32)
            return numerator / weight_sum
        return lax.map(one_head, query_group)
    result = lax.map(one_group, (query_heads, key_heads, value_heads))
    result = result.transpose(2, 0, 1, 3).reshape(TOKENS, HEADS * HEAD_DIM)
    result = jnp.where((position < length)[:, None], result, 0.0)
    return result.astype(jnp.bfloat16)
```

```python
import functools
import math

import jax
import jax.numpy as jnp
from jax import lax
from jax.experimental import pallas as pl
from jax.experimental.pallas import tpu as pltpu
from jax.sharding import PartitionSpec as P

HEADS = 32
KV_HEADS = 8
GROUP = 4
DIM = 128
SPAN = 128
EXP_SCALE = math.log2(math.e) / math.sqrt(DIM)
HIDDEN = -1e30
LIMIT = 2.0**110
CHUNKS = 4
TILE_BLOCKS = 4
NT = (((1,), (1,)), ((), ()))


def scores_t(keys, queries):
    return lax.dot_general(keys, queries, NT, preferred_element_type=jnp.float32)


def weights_of(scores):
    return jnp.exp2(scores * EXP_SCALE).astype(jnp.bfloat16)


def with_ones(values_t):
    ones = jnp.ones((16, values_t.shape[1]), jnp.bfloat16)
    return jnp.concatenate([values_t, ones], axis=0)


def attend(me_ref, q_ref, kv_ref, hide_ref, live_ref, o_ref, slot_ref, qx_ref, *acc_refs):
    me = me_ref[0]
    blocks, rows = kv_ref.shape[0], kv_ref.shape[3]
    spans = rows // SPAN
    tile_rows = TILE_BLOCKS * rows

    row = lax.broadcasted_iota(jnp.int32, (SPAN, SPAN), 0)
    lane = lax.broadcasted_iota(jnp.int32, (SPAN, SPAN), 1)

    @pl.when(pl.program_id(0) == 0)
    def _():
        for t in range(blocks * spans):
            slot_ref[t] = jnp.where((lane == 0) | (lane == 1 + t), 1.0, 0.0).astype(jnp.bfloat16)

    def keys_of(b):
        return kv_ref[b, 0, 0]

    def values_of(b):
        return [kv_ref[b, 1, 0, t * SPAN : (t + 1) * SPAN] for t in range(spans)]

    def slots_of(b):
        return [slot_ref[b * spans + t] for t in range(spans)]

    own_keys = keys_of(me)
    own_values = values_of(me)
    for i in range(GROUP):
        for t in range(spans):
            cut = slice(t * SPAN, (t + 1) * SPAN)
            q = q_ref[cut, i * DIM : (i + 1) * DIM]
            keys = own_keys[cut]
            near = jnp.where(lane <= row, scores_t(q, keys), HIDDEN)
            best = jnp.max(near, axis=1, keepdims=True).astype(jnp.bfloat16)
            extra = jnp.where(lane == 0, -best.astype(jnp.float32), hide_ref[cut].astype(jnp.float32))
            qx_ref[i, cut, :DIM] = q
            qx_ref[i, cut, DIM:] = extra.astype(jnp.bfloat16)
            first = jnp.where(lane == 0, 1.0, 0.0).astype(jnp.bfloat16)
            keys_x = jnp.concatenate([keys, first], axis=1)
            shifted = scores_t(keys_x, qx_ref[i, cut])
            weights = weights_of(jnp.where(row <= lane, shifted, HIDDEN))
            acc_refs[i][:, cut] = jnp.dot(
                with_ones(own_values[t]), weights, preferred_element_type=jnp.float32
            )

    @pl.loop(0, blocks // TILE_BLOCKS)
    def _(tile):
        first = tile * TILE_BLOCKS
        keys = jnp.concatenate([keys_of(first + b) for b in range(TILE_BLOCKS)], axis=0)
        slots = jnp.concatenate(
            [s for b in range(TILE_BLOCKS) for s in slots_of(first + b)], axis=0
        )
        keys_x = jnp.concatenate([keys, slots], axis=1)
        values_t = with_ones(
            jnp.concatenate([v for b in range(TILE_BLOCKS) for v in values_of(first + b)], axis=1)
        )

        def add(i, weights):
            acc_refs[i][...] += jnp.dot(values_t, weights, preferred_element_type=jnp.float32)

        held = None
        for i in range(GROUP):
            weights = weights_of(scores_t(keys_x, qx_ref[i]))
            if held is not None:
                add(i - 1, held)
            held = weights
        add(GROUP - 1, held)

    live = live_ref[0:1]

    def finish(i):
        acc = acc_refs[i][...]
        out = jnp.where(live > 0.0, acc[:DIM] / acc[DIM : DIM + 1], 0.0)
        o_ref[:, i * DIM : (i + 1) * DIM] = out.T.astype(jnp.bfloat16)

    top = acc_refs[0][DIM : DIM + 1]
    for i in range(1, GROUP):
        top = jnp.where(acc_refs[i][DIM : DIM + 1] < LIMIT, top, jnp.inf)
    good = jnp.min(jnp.where(top < LIMIT, 1.0, 0.0)) > 0.0

    for i in range(GROUP):
        finish(i)

    @pl.when(jnp.logical_not(good))
    def _():
        for i in range(GROUP):
            parts = []
            for t in range(spans):
                cut = slice(t * SPAN, (t + 1) * SPAN)
                near = scores_t(own_keys[cut], q_ref[cut, i * DIM : (i + 1) * DIM])
                near = jnp.where(row <= lane, near, HIDDEN)
                best = jnp.max(near, axis=0, keepdims=True)
                acc_refs[i][:, cut] = jnp.dot(
                    with_ones(own_values[t]), weights_of(near - best), preferred_element_type=jnp.float32
                )
                qx_ref[i, cut, DIM:] = jnp.where(
                    lane == 0, 0.0, hide_ref[cut].astype(jnp.float32)
                ).astype(jnp.bfloat16)
                parts.append(best)

            def absorb(b, best):
                keys_x = jnp.concatenate([keys_of(b), jnp.concatenate(slots_of(b), axis=0)], axis=1)
                scores = scores_t(keys_x, qx_ref[i])
                new = jnp.maximum(best, jnp.max(scores, axis=0, keepdims=True))
                values_t = with_ones(jnp.concatenate(values_of(b), axis=1))
                acc_refs[i][...] = acc_refs[i][...] * jnp.exp2((best - new) * EXP_SCALE) + jnp.dot(
                    values_t, weights_of(scores - new), preferred_element_type=jnp.float32
                )
                return new

            lax.fori_loop(0, blocks, absorb, jnp.concatenate(parts, axis=1))
            finish(i)


def shards(queries, keys_values, fold, doc_length):
    size = lax.axis_size("ctx")
    me = lax.axis_index("ctx")
    rows = queries.shape[0]
    spans = rows // SPAN
    slots = fold.shape[0]

    split = keys_values.reshape(rows, 2, KV_HEADS, DIM)
    keys = split[:, 0].transpose(1, 0, 2)
    values = split[:, 1].reshape(spans, SPAN, KV_HEADS, DIM).transpose(2, 0, 3, 1)
    packed = jnp.stack([keys, values.reshape(KV_HEADS, rows, DIM)])

    own = lax.dynamic_slice(fold, (me * spans,), (spans,))
    own_span = jnp.repeat(own, SPAN)
    hidden = fold[None, :] >= own_span[:, None]
    hide = jnp.where(hidden, HIDDEN, 0.0).astype(jnp.bfloat16)
    hide = jnp.pad(hide, ((0, 0), (1, DIM - 1 - slots)))
    position = own_span * SPAN + jnp.arange(rows, dtype=jnp.int32) % SPAN
    live = jnp.where(position < doc_length[0], 1.0, 0.0)
    live = jnp.broadcast_to(live[None, :], (8, rows))

    heads = KV_HEADS // CHUNKS
    call = pl.pallas_call(
        attend,
        grid_spec=pltpu.PrefetchScalarGridSpec(
            num_scalar_prefetch=1,
            grid=(heads,),
            in_specs=[
                pl.BlockSpec((rows, GROUP * DIM), lambda g, s: (0, s[1] * heads + g)),
                pl.BlockSpec((size, 2, 1, rows, DIM), lambda g, s: (0, 0, g, 0, 0)),
                pl.BlockSpec((rows, DIM), lambda g, s: (0, 0)),
                pl.BlockSpec((8, rows), lambda g, s: (0, 0)),
            ],
            out_specs=pl.BlockSpec((rows, GROUP * DIM), lambda g, s: (0, g)),
            scratch_shapes=[
                pltpu.VMEM((slots, SPAN, DIM), jnp.bfloat16),
                pltpu.VMEM((GROUP, rows, 2 * DIM), jnp.bfloat16),
            ]
            + [pltpu.VMEM((DIM + 16, rows), jnp.float32)] * GROUP,
        ),
        out_shape=jax.ShapeDtypeStruct((rows, heads * GROUP * DIM), jnp.bfloat16),
        compiler_params=pltpu.CompilerParams(vmem_limit_bytes=40 * 2**20),
        cost_estimate=pl.CostEstimate(
            flops=4 * rows * size * rows * heads * GROUP * DIM,
            transcendentals=rows * size * rows * heads * GROUP,
            bytes_accessed=size * 4 * heads * rows * DIM,
        ),
    )
    outs = []
    for c in range(CHUNKS):
        whole = lax.all_gather(packed[:, c * heads : (c + 1) * heads], "ctx")
        outs.append(call(jnp.stack([me, c]), queries, whole, hide, live))
    return jnp.concatenate(outs, axis=1)


def solution(mesh):
    in_specs = (P(("dp", "ctx"), None), P(("dp", "ctx"), None, None), P("dp"), P("dp"))
    out_specs = P(("dp", "ctx"), None)
    return jax.shard_map(shards, mesh=mesh, in_specs=in_specs, out_specs=out_specs, check_vma=False)
```

```python
import functools
import math

import jax
import jax.numpy as jnp
from jax import lax
from jax.experimental import pallas as pl
from jax.experimental.pallas import tpu as pltpu
from jax.sharding import PartitionSpec as P

KV_HEADS = 8
GROUP = 4
DIM = 128
SPAN = 128
BLOCKS = 16
PIECES = 4
PAIR = KV_HEADS // PIECES
RING = 4
EXP_SCALE = math.log2(math.e) / math.sqrt(DIM)
HIDDEN = -1e30
LIMIT = 2.0**110
SENDS = 60
NT = (((1,), (1,)), ((), ()))
MESH = pl.DeviceIdType.MESH


def scores_t(keys, queries):
    return lax.dot_general(keys, queries, NT, preferred_element_type=jnp.float32)


def weights_of(scores):
    return jnp.exp2(scores * EXP_SCALE).astype(jnp.bfloat16)


def with_ones(values_t):
    ones = jnp.ones((16, values_t.shape[1]), jnp.bfloat16)
    return jnp.concatenate([values_t, ones], axis=0)


def halves(block):
    return [block[t * SPAN : (t + 1) * SPAN] for t in range(block.shape[0] // SPAN)]


def gather_attend(
    q_hbm, own_hbm, hide_ref, *refs
):
    acc_refs, whole_hbm = refs[:GROUP], refs[GROUP]
    buf, q_ref, qx_ref, slot_ref, send_sem, recv_sem, own_sem, out_sem = refs[GROUP + 1 :]
    me = lax.axis_index("ctx")
    core = me % 2
    x = (me // 2) % RING
    y = me // (2 * RING)
    x_right, x_left, x_far = (x + 1) % RING, (x + 3) % RING, (x + 2) % RING
    y_far = 1 - y
    rows = q_ref.shape[0]
    spans = rows // SPAN

    def block_at(row, column):
        return (row * RING + column) * 2 + core

    right, left = block_at(y, x_right), block_at(y, x_left)
    partner, sibling = block_at(y_far, x), (y * RING + x) * 2 + 1 - core
    far = block_at(y, x_far)
    partner_left, partner_right = block_at(y_far, x_left), block_at(y_far, x_right)
    partner_far = block_at(y_far, x_far)

    barrier = pltpu.get_barrier_semaphore()
    for other in (right, left, partner, sibling):
        pl.semaphore_signal(barrier, inc=1, device_id={"ctx": other}, device_id_type=MESH)

    q_copy = pltpu.make_async_copy(q_hbm, q_ref, own_sem.at[0])
    own_copy = pltpu.make_async_copy(own_hbm, buf.at[me], own_sem.at[1])
    q_copy.start()
    own_copy.start()

    count = [0]

    def send(block, piece, target, source=None):
        pltpu.make_async_remote_copy(
            src_ref=buf.at[block, piece] if source is None else source,
            dst_ref=buf.at[block, piece],
            send_sem=send_sem.at[count[0]],
            recv_sem=recv_sem.at[block, piece],
            device_id={"ctx": target},
            device_id_type=MESH,
        ).start()
        count[0] += 1

    def arrived(block, piece):
        pltpu.make_async_remote_copy(
            src_ref=buf.at[block, piece],
            dst_ref=buf.at[block, piece],
            send_sem=send_sem.at[0],
            recv_sem=recv_sem.at[block, piece],
            device_id={"ctx": sibling},
            device_id_type=MESH,
        ).wait_recv()

    pl.semaphore_wait(barrier, 4)
    for j in range(PIECES):
        k = (j + 2) % PIECES
        send(me, j, right, own_hbm.at[j])
        send(me, k, left, own_hbm.at[k])
        send(me, k, partner, own_hbm.at[k])
        send(me, j, sibling, own_hbm.at[j])

    row = lax.broadcasted_iota(jnp.int32, (SPAN, SPAN), 0)
    lane = lax.broadcasted_iota(jnp.int32, (SPAN, SPAN), 1)
    for t in range(BLOCKS * spans):
        slot_ref[t] = jnp.where((lane == 0) | (lane == 1 + t), 1.0, 0.0).astype(jnp.bfloat16)
    q_copy.wait()
    own_copy.wait()

    @pl.loop(0, KV_HEADS)
    def _(g):
        piece, pair = g // PAIR, g % PAIR
        own_keys = buf[me, piece, 0, pair]
        own_values = halves(buf[me, piece, 1, pair])
        q_all = q_ref[:, pl.ds(pl.multiple_of(g * GROUP * DIM, GROUP * DIM), GROUP * DIM)]
        for i in range(GROUP):
            for t in range(spans):
                cut = slice(t * SPAN, (t + 1) * SPAN)
                q = q_all[cut, i * DIM : (i + 1) * DIM]
                keys = own_keys[cut]
                near = jnp.where(lane <= row, scores_t(q, keys), HIDDEN)
                best = jnp.max(near, axis=1, keepdims=True).astype(jnp.bfloat16)
                extra = jnp.where(
                    lane == 0, -best.astype(jnp.float32), hide_ref[cut].astype(jnp.float32)
                )
                q_x = jnp.concatenate([q, extra.astype(jnp.bfloat16)], axis=1)
                qx_ref[g, i, cut] = q_x
                first = jnp.where(lane == 0, 1.0, 0.0).astype(jnp.bfloat16)
                keys_x = jnp.concatenate([keys, first], axis=1)
                weights = weights_of(jnp.where(row <= lane, scores_t(keys_x, q_x), HIDDEN))
                acc_refs[i][g, :, cut] = jnp.dot(
                    with_ones(own_values[t]), weights, preferred_element_type=jnp.float32
                )

    def take(*pieces):
        for block, piece in pieces:
            arrived(block, piece)
            send(block, piece, sibling)

    def stage_0():
        take((left, 0), (right, 2), (partner, 2))
        send(left, 0, right)
        send(right, 2, left)
        take((left, 1), (right, 3), (partner, 3))
        send(left, 1, right)
        send(right, 3, left)
        for piece in (2, 3):
            send(partner, piece, right)
            send(partner, piece, left)

    def stage_1():
        take((left, 2), (right, 0), (partner, 0))
        send(partner, 0, right)
        send(partner, 0, left)

    def stage_2():
        take((left, 3), (right, 1), (partner, 1))
        send(partner, 1, right)
        send(partner, 1, left)

    def stage_3():
        for piece in (0, 2):
            take((far, piece))
            send(far, piece, partner)

    def stage_4():
        for piece in (1, 3):
            take((far, piece))
            send(far, piece, partner)
        take((partner_far, 0), (partner_left, 2), (partner_right, 2), (partner_far, 2))

    def stage_5():
        take((partner_left, 3), (partner_right, 3), (partner_far, 1))

    def stage_6():
        take((partner_left, 0), (partner_right, 0), (partner_far, 3))

    def stage_7():
        take((partner_left, 1), (partner_right, 1))

    stages = (stage_0, stage_1, stage_2, stage_3, stage_4, stage_5, stage_6, stage_7)

    def kept(block, piece, n):
        return pltpu.make_async_copy(buf.at[block, piece], whole_hbm.at[block, piece], out_sem.at[n])

    def pick(condition, a, b):
        return jnp.where(condition, a, b)

    def step(w, carry):
        for n, stage in enumerate(stages):
            pl.when(w == n)(stage)

        def tile(t, carry):
            late, second = w >= len(stages) // 2, t == 1
            turned = (w + 2) % PIECES
            swapped = (w % PIECES) // 2 + 2 * (w % 2)
            piece = pick(second, turned, pick(late, swapped, w % PIECES))
            one = pick(second, pick(late, partner_left, partner), pick(late, far, me))
            two = pick(second, pick(late, partner_right, right), pick(late, partner_far, left))
            other = 1 - 2 * core
            arrived(one + other, piece)
            arrived(two + other, piece)
            blocks = (one, one + other, two, two + other)
            for j, b in enumerate(blocks):
                kept(b, piece, (w * 2 + t) * 4 + j).start()

            def key_head(pair, carry):
                g = piece * PAIR + pair
                keys = jnp.concatenate([buf[b, piece, 0, pair] for b in blocks], axis=0)
                slots = jnp.concatenate(
                    [slot_ref[b * spans + s] for b in blocks for s in range(spans)], axis=0
                )
                keys_x = jnp.concatenate([keys, slots], axis=1)
                values_t = with_ones(
                    jnp.concatenate([v for b in blocks for v in halves(buf[b, piece, 1, pair])], axis=1)
                )

                def add(i, weights):
                    acc_refs[i][g] += jnp.dot(values_t, weights, preferred_element_type=jnp.float32)

                held = None
                for i in range(GROUP):
                    weights = weights_of(scores_t(keys_x, qx_ref[g, i]))
                    if held is not None:
                        add(i - 1, held)
                    held = weights
                add(GROUP - 1, held)
                return carry

            return lax.fori_loop(0, PAIR, key_head, carry)

        return lax.fori_loop(0, 2, tile, carry)

    lax.fori_loop(0, len(stages), step, 0)

    def drain(n, carry):
        pltpu.make_async_remote_copy(
            src_ref=buf.at[me, 0],
            dst_ref=buf.at[me, 0],
            send_sem=send_sem.at[n],
            recv_sem=recv_sem.at[me, 0],
            device_id={"ctx": sibling},
            device_id_type=MESH,
        ).wait_send()
        return carry

    assert count[0] == SENDS
    lax.fori_loop(0, SENDS, drain, 0)

    def drain_kept(n, carry):
        kept(me, 0, n).wait()
        return carry

    lax.fori_loop(0, BLOCKS * PIECES, drain_kept, 0)


def finish_attend(q_ref, hide_ref, live_ref, *refs):
    acc_in, (whole_hbm, o_ref, kv_ref, qx_ref, acc_ref, sem) = refs[:GROUP], refs[GROUP:]
    g = pl.program_id(0)
    me = lax.axis_index("ctx")
    rows = q_ref.shape[0]
    spans = rows // SPAN
    row = lax.broadcasted_iota(jnp.int32, (SPAN, SPAN), 0)
    lane = lax.broadcasted_iota(jnp.int32, (SPAN, SPAN), 1)
    live = live_ref[0:1]

    def finish(i, acc):
        out = jnp.where(live > 0.0, acc[:DIM] / acc[DIM : DIM + 1], 0.0)
        o_ref[:, i * DIM : (i + 1) * DIM] = out.T.astype(jnp.bfloat16)

    good = jnp.where(acc_in[0][0, DIM : DIM + 1] < LIMIT, 1.0, 0.0)
    for i in range(1, GROUP):
        good = jnp.where(acc_in[i][0, DIM : DIM + 1] < LIMIT, good, 0.0)
    for i in range(GROUP):
        finish(i, acc_in[i][0])

    @pl.when(jnp.min(good) < 0.5)
    def _():
        def fetch(b):
            copy = pltpu.make_async_copy(whole_hbm.at[b, g // PAIR, :, g % PAIR], kv_ref, sem)
            copy.start()
            copy.wait()

        for i in range(GROUP):
            fetch(me)
            parts = []
            for t in range(spans):
                cut = slice(t * SPAN, (t + 1) * SPAN)
                q = q_ref[cut, i * DIM : (i + 1) * DIM]
                near = jnp.where(row <= lane, scores_t(kv_ref[0, cut], q), HIDDEN)
                best = jnp.max(near, axis=0, keepdims=True)
                acc_ref[:, cut] = jnp.dot(
                    with_ones(kv_ref[1, cut]), weights_of(near - best), preferred_element_type=jnp.float32
                )
                extra = jnp.where(lane == 0, 0.0, hide_ref[cut].astype(jnp.float32))
                qx_ref[cut] = jnp.concatenate([q, extra.astype(jnp.bfloat16)], axis=1)
                parts.append(best)

            def absorb(b, best):
                fetch(b)
                key_row = lax.broadcasted_iota(jnp.int32, (rows, DIM), 0)
                slot = lax.broadcasted_iota(jnp.int32, (rows, DIM), 1) - 1 - b * spans
                slots = jnp.where(key_row // SPAN == slot, 1.0, 0.0).astype(jnp.bfloat16)
                scores = scores_t(jnp.concatenate([kv_ref[0], slots], axis=1), qx_ref[...])
                new = jnp.maximum(best, jnp.max(scores, axis=0, keepdims=True))
                values_t = with_ones(jnp.concatenate(halves(kv_ref[1]), axis=1))
                acc_ref[...] = acc_ref[...] * jnp.exp2((best - new) * EXP_SCALE) + jnp.dot(
                    values_t, weights_of(scores - new), preferred_element_type=jnp.float32
                )
                return new

            lax.fori_loop(0, BLOCKS, absorb, jnp.concatenate(parts, axis=1))
            finish(i, acc_ref[...])


def shards(queries, keys_values, fold, doc_length):
    me = lax.axis_index("ctx")
    rows = queries.shape[0]
    spans = rows // SPAN
    slots = fold.shape[0]

    split = keys_values.reshape(rows, 2, PIECES, PAIR, DIM)
    keys = split[:, 0].transpose(1, 2, 0, 3)
    values = split[:, 1].reshape(spans, SPAN, PIECES, PAIR, DIM).transpose(2, 3, 0, 4, 1)
    packed = jnp.stack([keys, values.reshape(PIECES, PAIR, rows, DIM)], axis=1)

    own = lax.dynamic_slice(fold, (me * spans,), (spans,))
    own_span = jnp.repeat(own, SPAN)
    hidden = fold[None, :] >= own_span[:, None]
    hide = jnp.where(hidden, HIDDEN, 0.0).astype(jnp.bfloat16)
    hide = jnp.pad(hide, ((0, 0), (1, DIM - 1 - slots)))
    position = own_span * SPAN + jnp.arange(rows, dtype=jnp.int32) % SPAN
    live = jnp.where(position < doc_length[0], 1.0, 0.0)
    live = jnp.broadcast_to(live[None, :], (8, rows))

    anywhere = pl.BlockSpec(memory_space=pl.ANY)
    in_vmem = pl.BlockSpec(memory_space=pltpu.VMEM)
    sums = jax.ShapeDtypeStruct((KV_HEADS, DIM + 16, rows), jnp.float32)
    whole = jax.ShapeDtypeStruct((BLOCKS, PIECES, 2, PAIR, rows, DIM), jnp.bfloat16)
    *accs, gathered = pl.pallas_call(
        gather_attend,
        in_specs=[anywhere, anywhere, in_vmem],
        out_specs=[in_vmem] * GROUP + [anywhere],
        out_shape=[sums] * GROUP + [whole],
        scratch_shapes=[
            pltpu.VMEM(whole.shape, jnp.bfloat16),
            pltpu.VMEM(queries.shape, jnp.bfloat16),
            pltpu.VMEM((KV_HEADS, GROUP, rows, 2 * DIM), jnp.bfloat16),
            pltpu.VMEM((slots, SPAN, DIM), jnp.bfloat16),
            pltpu.SemaphoreType.DMA((SENDS,)),
            pltpu.SemaphoreType.DMA((BLOCKS, PIECES)),
            pltpu.SemaphoreType.DMA((2,)),
            pltpu.SemaphoreType.DMA((BLOCKS * PIECES,)),
        ],
        compiler_params=pltpu.CompilerParams(
            collective_id=0, has_side_effects=True, vmem_limit_bytes=48 * 2**20
        ),
    )(queries, packed, hide)

    return pl.pallas_call(
        finish_attend,
        grid=(KV_HEADS,),
        in_specs=[
            pl.BlockSpec((rows, GROUP * DIM), lambda g: (0, g)),
            pl.BlockSpec((rows, DIM), lambda g: (0, 0)),
            pl.BlockSpec((8, rows), lambda g: (0, 0)),
        ]
        + [pl.BlockSpec((1, DIM + 16, rows), lambda g: (g, 0, 0))] * GROUP
        + [anywhere],
        out_specs=pl.BlockSpec((rows, GROUP * DIM), lambda g: (0, g)),
        out_shape=jax.ShapeDtypeStruct(queries.shape, jnp.bfloat16),
        scratch_shapes=[
            pltpu.VMEM((2, rows, DIM), jnp.bfloat16),
            pltpu.VMEM((rows, 2 * DIM), jnp.bfloat16),
            pltpu.VMEM((DIM + 16, rows), jnp.float32),
            pltpu.SemaphoreType.DMA,
        ],
        compiler_params=pltpu.CompilerParams(vmem_limit_bytes=24 * 2**20),
    )(queries, hide, live, *accs, gathered)


def solution(mesh):
    in_specs = (P(("dp", "ctx"), None), P(("dp", "ctx"), None, None), P("dp"), P("dp"))
    out_specs = P(("dp", "ctx"), None)
    return jax.shard_map(shards, mesh=mesh, in_specs=in_specs, out_specs=out_specs, check_vma=False)
```
